256 devices in a mesh: client: 32 (over x, z), feat: 8 (over y, core).
Axes of the slice: x: 4, y: 4, z: 8, core: 2. Of those that a mesh axis runs over, the one named last changes fastest.
Arguments:
- bin_codes: int32 [512, 49152], P('feat', 'client'), may hold values from 0 to 255
- node_ids: int32 [49152], P('client'), may hold values from 0 to 7
- margins: float32 [16, 49152], P(None, 'client'), may hold values from -1 to 3
- labels: float32 [16, 49152], P(None, 'client'), may hold values from 0 to 1
- split_feature: int32 [8], replicated, may hold values from 0 to 511
- split_bin: int32 [8], replicated, may hold values from 0 to 254
Outputs:
- split_gains: float32 [8, 512, 256], P(None, ('feat', 'client'))
- leaf_weights: float32 [16, 16], replicated
- new_margins: float32 [16, 49152], P(None, 'client')
The draws below stay inside these ranges and needn't reach their ends.
All inputs are finite; a program needn't handle non-finite values.
Results may differ from the reference program's by a relative error of at most 0.0039.
Values may be sent and summed in bfloat16 or wider, within the bound.
A program may use at most 64 MiB of HBM per device.

```python
import jax
import jax.numpy as jnp
from jax import lax

F = 512
BINS = 256
TARGETS = 16
NODES = 8
ROWS = 49152


def place_ends(array, key, smallest, top_value):
    extent = array.shape
    place = [jax.random.randint(jax.random.fold_in(key, axis), (), 0, extent[axis]) for axis in range(len(extent))]
    array = array.at[tuple(place)].set(smallest)
    longest = extent.index(max(extent))
    place[longest] = (place[longest] + 1) % extent[longest]
    return array.at[tuple(place)].set(top_value)


def block_scale(stream_key, dims, split, low, top_value):
    gain = 1.0
    for dim, blocks in split:
        steps = jax.random.uniform(jax.random.fold_in(jax.random.fold_in(stream_key, 6), dim), (blocks,), jnp.float32, low / len(split), top_value / len(split))
        gain = gain * jnp.repeat(jnp.exp(steps), dims[dim] // blocks).reshape((-1,) + (1,) * (len(dims) - 1 - dim))
    return gain


def setup_inputs(seed: int = 0) -> dict:
    seeds = jax.random.split(jax.random.key(seed), 7)
    bin_codes = place_ends(jax.random.randint(seeds[0], (F, ROWS), 0, BINS), jax.random.fold_in(seeds[0], 1), 0, BINS - 1).astype(jnp.int32)
    node_ids = place_ends(jax.random.randint(seeds[1], (ROWS,), 0, NODES), jax.random.fold_in(seeds[1], 1), 0, NODES - 1).astype(jnp.int32)
    margins = jnp.clip(-1.0 + 4.0 * jax.random.uniform(seeds[2], (TARGETS, ROWS), jnp.float32) ** block_scale(seeds[2], (TARGETS, ROWS), ((1, 32),), -0.2, 0.2), -1.0, 3.0)
    labels = jnp.clip(1.0 * jax.random.uniform(seeds[3], (TARGETS, ROWS), jnp.float32) ** block_scale(seeds[3], (TARGETS, ROWS), ((1, 32),), -0.2, 0.2), 0.0, 1.0)
    split_feature = place_ends(jax.random.randint(seeds[4], (NODES,), 0, F), jax.random.fold_in(seeds[4], 1), 0, F - 1).astype(jnp.int32)
    split_bin = place_ends(jax.random.randint(seeds[5], (NODES,), 0, BINS - 1), jax.random.fold_in(seeds[5], 1), 0, (BINS - 1) - 1).astype(jnp.int32)
    return dict(bin_codes=bin_codes, node_ids=node_ids, margins=margins, labels=labels, split_feature=split_feature, split_bin=split_bin)


reg_lambda = 1.0
step_eta = 0.5


def gain_table(prefix, targets):
    left_grad = prefix[..., :targets]
    left_hess = prefix[..., targets:]
    total_grad = prefix[:, -1:, :, :targets]
    total_hess = prefix[:, -1:, :, targets:]
    value = left_grad * left_grad / (left_hess + reg_lambda)
    value = value + (total_grad - left_grad) ** 2 / (total_hess - left_hess + reg_lambda)
    value = value - total_grad * total_grad / (total_hess + reg_lambda)
    return 0.5 * jnp.sum(value, axis=-1)


def leaf_table(left_sums, node_sums, targets):
    left_grad = left_sums[:, :targets]
    left_hess = left_sums[:, targets:]
    total_grad = node_sums[:, :targets]
    total_hess = node_sums[:, targets:]
    left_weight = -left_grad / (left_hess + reg_lambda)
    right_weight = -(total_grad - left_grad) / (total_hess - left_hess + reg_lambda)
    return jnp.stack([left_weight, right_weight], axis=1).reshape(2 * left_sums.shape[0], targets)


def reference(bin_codes, node_ids, margins, labels, split_feature, split_bin):
    probability = jax.nn.sigmoid(margins)
    gradient = (probability - labels).astype(jnp.bfloat16)
    hessian = (probability * (1.0 - probability)).astype(jnp.bfloat16)
    row_stats = jnp.concatenate([gradient, hessian], axis=0).T.astype(jnp.float32)

    def per_feature(column):
        segment = column * NODES + node_ids
        return jax.ops.segment_sum(row_stats, segment, num_segments=BINS * NODES)

    histogram = lax.map(per_feature, bin_codes).reshape(F, BINS, NODES, 2 * TARGETS)
    prefix = jnp.cumsum(histogram, axis=1)
    split_gains = gain_table(prefix, TARGETS).transpose(2, 0, 1)
    node_index = jnp.arange(NODES, dtype=jnp.int32)
    left_sums = prefix[split_feature, split_bin, node_index]
    node_sums = prefix[split_feature, BINS - 1, node_index]
    leaf_weights = leaf_table(left_sums, node_sums, TARGETS)
    row_index = jnp.arange(ROWS, dtype=jnp.int32)
    row_code = bin_codes[split_feature[node_ids], row_index]
    child = 2 * node_ids + (row_code > split_bin[node_ids]).astype(jnp.int32)
    new_margins = margins + step_eta * leaf_weights[child].T
    return split_gains, leaf_weights, new_margins
```

```python
import jax
import jax.numpy as jnp
from jax import lax
from jax.experimental import pallas as pl
from jax.experimental.pallas import tpu as pltpu
from jax.sharding import PartitionSpec as P

F32 = jnp.float32
BF16 = jnp.bfloat16
MESH = pl.DeviceIdType.MESH
BINS = 256
NODES = 8
TARGETS = 16
CH = 2 * TARGETS
X, Y, Z = 4, 4, 8
CLIENTS = X * Z
FEATS = 2 * Y
ROWS = 1536
QUARTER = ROWS // Y
HALF = ROWS // 2
SLAB = 64
OWNED = 2
reg_lambda = 1.0
step_eta = 0.5
CONTRACT_LAST = (((1,), (1,)), ((), ()))


def split3(a):
    hi = a.astype(BF16)
    rest = a - hi.astype(F32)
    mid = rest.astype(BF16)
    low = (rest - mid.astype(F32)).astype(BF16)
    return hi, mid, low


def dot3(a, b):
    hi, mid, low = split3(a)
    out = jnp.dot(low, b, preferred_element_type=F32)
    out = out + jnp.dot(mid, b, preferred_element_type=F32)
    return out + jnp.dot(hi, b, preferred_element_type=F32)


def remote(src, dst, send, recv, client, feat):
    return pltpu.make_async_remote_copy(
        src_ref=src,
        dst_ref=dst,
        send_sem=send,
        recv_sem=recv,
        device_id=(client, feat),
        device_id_type=MESH,
    )


def kernel(
    split_feature,
    split_bin,
    codes,
    node_ids,
    margins,
    labels,
    gains_out,
    leaf_out,
    margins_out,
    msg,
    codes_all,
    stats,
    pieces,
    sides,
    sums,
    acc,
    ss_codes,
    rs_codes,
    ss_side,
    rs_side,
    ss_sums,
    rs_sums,
    ss_z,
    rs_z,
    ss_piece,
    rs_piece,
):
    me = lax.axis_index("client")
    feat = lax.axis_index("feat")
    x = me // Z
    z = me % Z
    y = feat // 2
    k = feat % 2
    kp = z % 2
    zz_own = z // 2

    barrier = pltpu.get_barrier_semaphore()

    def greet_client(j, carry):
        pl.semaphore_signal(
            barrier, inc=1, device_id=((me + j) % CLIENTS, feat), device_id_type=MESH
        )
        return carry

    def greet_feat(j, carry):
        pl.semaphore_signal(
            barrier, inc=1, device_id=(me, (feat + j) % FEATS), device_id_type=MESH
        )
        return carry

    lax.fori_loop(1, CLIENTS, greet_client, 0)
    lax.fori_loop(1, FEATS, greet_feat, 0)

    node = node_ids[...]

    node_f = node.astype(F32)
    node_pair = jnp.concatenate([node_f[:, :HALF], node_f[:, HALF:]], axis=0).astype(BF16)

    def fill(q, carry):
        block = codes[pl.ds(pl.multiple_of(8 * q, 8), 8), :].astype(F32)
        for i in range(4):
            pair = block[OWNED * i : OWNED * (i + 1)].astype(BF16)
            msg[4 * q + i, 0] = pair[:, :HALF]
            msg[4 * q + i, 1] = pair[:, HALF:]
            msg[4 * q + i, 2] = node_pair
        return carry

    lax.fori_loop(0, CLIENTS // 4, fill, 0)

    probability = 1.0 / (1.0 + jnp.exp(-margins[...]))
    stats[0:TARGETS, :] = (probability - labels[...]).astype(BF16)
    stats[TARGETS:CH, :] = (probability * (1.0 - probability)).astype(BF16)

    side = jnp.zeros((1, ROWS), F32)
    for n in range(NODES):
        column = split_feature[n] - feat * SLAB
        held = jnp.where((column >= 0) & (column < SLAB), 1.0, 0.0)
        row = codes[pl.ds(jnp.clip(column, 0, SLAB - 1), 1), :]
        right = jnp.where((row > split_bin[n]) & (node == n), 1.0, 0.0)
        side = side + held * right
    sides[feat] = jnp.concatenate([side[:, :HALF], side[:, HALF:]], axis=0).astype(BF16)

    def piece_at(ra, rb, par):
        ax = ra * (1 - par) + rb * par
        ay = ra * par + rb * (1 - par)
        px = (x + ax) % X
        quarter = (y + ay) % Y
        return px, quarter, (quarter * X + px) * 2 + par

    first = piece_at(0, 0, k)[2]

    @pl.when(k == kp)
    def _():
        pieces[first, zz_own] = stats[:, pl.ds(pl.multiple_of(y * QUARTER, 128), QUARTER)]

    pl.semaphore_wait(barrier, CLIENTS - 1 + FEATS - 1)

    def z_copy(j):
        to = (z + j) % Z
        return remote(
            pieces.at[first, zz_own],
            pieces.at[first, zz_own],
            ss_z.at[to],
            rs_z.at[zz_own],
            x * Z + to,
            feat,
        )

    @pl.when(k == kp)
    def _():
        for j in (4, 3, 5, 2, 6, 1, 7):
            z_copy(j).start()

    def side_copy(j):
        to = (feat + j) % FEATS
        return remote(sides.at[feat], sides.at[feat], ss_side.at[to], rs_side.at[feat], me, to)

    for j in range(1, FEATS):
        side_copy(j).start()

    def codes_copy(j):
        to = (me + j) % CLIENTS
        return remote(msg.at[to], codes_all.at[me], ss_codes.at[to], rs_codes.at[me], to, feat)

    def send_codes(j, carry):
        codes_copy(j).start()
        return carry

    lax.fori_loop(1, CLIENTS, send_codes, 0)
    own_codes = pltpu.make_async_copy(msg.at[me], codes_all.at[me], rs_codes.at[me])
    own_codes.start()

    for j in range(1, FEATS):
        frm = (feat + j) % FEATS
        remote(sides.at[frm], sides.at[frm], ss_side.at[frm], rs_side.at[frm], me, frm).wait_recv()
    side_pair = sides[0].astype(F32)
    for j in range(1, FEATS):
        side_pair = side_pair + sides[j].astype(F32)
    side = jnp.concatenate([side_pair[0:1], side_pair[1:2]], axis=1)
    child = 2 * node + side.astype(jnp.int32)
    node_iota = lax.broadcasted_iota(jnp.int32, (NODES, ROWS), 0)
    left_mask = jnp.where(2 * node_iota == child, 1.0, 0.0)
    node_mask = jnp.where(node_iota == node, 1.0, 0.0)
    mask = jnp.concatenate([left_mask, node_mask], axis=0).astype(BF16)
    part = lax.dot_general(mask, stats[...], CONTRACT_LAST, preferred_element_type=F32)
    sums[me] = jnp.concatenate(
        [part[:NODES], part[NODES:], jnp.zeros((NODES, 128 - 2 * CH), F32)], axis=1
    )

    def sums_copy(j):
        to = (me + j) % CLIENTS
        return remote(sums.at[me], sums.at[me], ss_sums.at[to], rs_sums.at[me], to, feat)

    def send_sums(j, carry):
        sums_copy(j).start()
        return carry

    lax.fori_loop(1, CLIENTS, send_sums, 0)

    def order(t):
        late = (t + 12) // 16
        last = (t + 4) // 16
        j = (1 - late) * t + late * (1 - last) * ((t - 4) // 2) + last * (t - 12)
        ra = j + j // 2 - 2 * (j // 3)
        rb = late * (1 - last) * (3 - 2 * (t % 2)) + 2 * last
        return ra, rb

    def along(da, db):
        ax = da * (1 - k) + db * k
        ay = da * k + db * (1 - k)
        return ((x + ax) % X) * Z + z, ((y + ay) % Y) * 2 + k

    def piece_copy(p, t, slot, client, to_feat):
        return remote(
            pieces.at[p], pieces.at[p], ss_piece.at[t * 5 + slot], rs_piece.at[p], client, to_feat
        )

    def piece_sends(t, act):
        ra, rb = order(t)
        p = piece_at(ra, rb, k)[2]
        act(piece_copy(p, t, 4, me, y * 2 + (1 - k)))

        @pl.when((rb == 0) & (ra == 0))
        def _():
            for slot, d in ((0, 1), (1, 3)):
                act(piece_copy(p, t, slot, *along(d, 0)))

        @pl.when((rb == 0) & (ra == 1))
        def _():
            act(piece_copy(p, t, 1, *along(3, 0)))

        @pl.when(rb == 0)
        def _():
            for slot, d in ((2, 1), (3, 3)):
                act(piece_copy(p, t, slot, *along(0, d)))

        @pl.when((rb == 3) & ((ra == 0) | (ra == 3)))
        def _():
            act(piece_copy(p, t, 2, *along(0, 1)))

        @pl.when((rb == 1) & ((ra == 1) | (ra == 2)))
        def _():
            act(piece_copy(p, t, 3, *along(0, 3)))

    def wait_piece(p):
        remote(
            pieces.at[p], pieces.at[p], ss_piece.at[0], rs_piece.at[p], me, y * 2 + (1 - k)
        ).wait_recv()

    def start(copy):
        copy.start()

    def wait_send(copy):
        copy.wait_send()

    for j in range(4):

        @pl.when(2 * j + k != z)
        def _():
            remote(
                pieces.at[first, j],
                pieces.at[first, j],
                ss_z.at[2 * j + k],
                rs_z.at[j],
                x * Z + 2 * j + k,
                feat,
            ).wait_recv()

    piece_sends(0, start)

    acc[...] = jnp.zeros_like(acc)

    def wait_codes(px, par):
        for j in range(4):
            frm = px * Z + 2 * j + par
            pltpu.make_async_copy(msg.at[frm], codes_all.at[frm], rs_codes.at[frm]).wait()

    def step(t, carry):
        @pl.when(t < 15)
        def _():
            ra, rb = order(t + 1)
            wait_piece(piece_at(ra, rb, k)[2])
            piece_sends(t + 1, start)

        ra, rb = order(t)
        code_list = []
        node_list = []
        stat_list = []
        for which in range(2):
            par = k * (1 - which) + (1 - k) * which
            px, quarter, p = piece_at(ra, rb, par)

            @pl.when(((1 - par) * rb + par * ra) == 0)
            def _():
                wait_codes(px, par)

            if which == 1:
                wait_piece(p)
            half = quarter // 2
            lanes = pl.ds(pl.multiple_of((quarter % 2) * QUARTER, 128), QUARTER)
            for j in range(4):
                frm = px * Z + 2 * j + par
                code_list.append(codes_all[frm, half, :, lanes].astype(F32))
                pair = codes_all[frm, 2, :, lanes].astype(F32)
                node_list.append(jnp.where(half == 0, pair[0:1], pair[1:2]))
                stat_list.append(pieces[p, j])
        code = jnp.concatenate(code_list, axis=1).astype(jnp.int32)
        nodes = jnp.concatenate(node_list, axis=1).astype(jnp.int32)
        stat = jnp.concatenate(stat_list, axis=1).astype(F32)
        width = code.shape[1]
        bin_iota = lax.broadcasted_iota(jnp.int32, (BINS, width), 0)
        onehot = jnp.concatenate(
            [jnp.where(code[f : f + 1] == bin_iota, 1.0, 0.0).astype(BF16) for f in range(OWNED)],
            axis=0,
        )
        spread = jnp.concatenate(
            [jnp.where(nodes == n, stat, 0.0).astype(BF16) for n in range(NODES)], axis=0
        )
        acc[...] += lax.dot_general(spread, onehot, CONTRACT_LAST, preferred_element_type=F32)
        return carry

    lax.fori_loop(0, 16, step, 0)

    def wait_sums(j, carry):
        frm = (me + j) % CLIENTS
        remote(sums.at[frm], sums.at[frm], ss_sums.at[frm], rs_sums.at[frm], frm, feat).wait_recv()
        return carry

    lax.fori_loop(1, CLIENTS, wait_sums, 0)
    total = jnp.sum(sums[...], axis=0)
    left = total[:, :CH]
    whole = total[:, CH : 2 * CH]
    right = whole - left
    left_weight = -left[:, :TARGETS] / (left[:, TARGETS:] + reg_lambda)
    right_weight = -right[:, :TARGETS] / (right[:, TARGETS:] + reg_lambda)
    rows = []
    for n in range(NODES):
        rows.append(left_weight[n : n + 1])
        rows.append(right_weight[n : n + 1])
    weights = jnp.concatenate(rows, axis=0)
    leaf_out[...] = weights
    columns = jnp.concatenate([weights, jnp.zeros((2 * NODES, 128 - TARGETS), F32)], axis=1).T
    child_iota = lax.broadcasted_iota(jnp.int32, (2 * NODES, ROWS), 0)
    child_mask = jnp.where(child_iota == child, 1.0, 0.0).astype(BF16)
    lookup = dot3(columns[:TARGETS, :], child_mask)
    margins_out[...] = margins[...] + step_eta * lookup

    row_bin = lax.broadcasted_iota(jnp.int32, (BINS, BINS), 0)
    col_bin = lax.broadcasted_iota(jnp.int32, (BINS, BINS), 1)
    upto = jnp.where(row_bin <= col_bin, 1.0, 0.0).astype(BF16)
    for f in range(OWNED):
        prefix = dot3(acc[:, f * BINS : (f + 1) * BINS], upto)
        for n in range(NODES):
            gl = prefix[n * CH : n * CH + TARGETS]
            hl = prefix[n * CH + TARGETS : (n + 1) * CH]
            g = gl[:, BINS - 1 :]
            h = hl[:, BINS - 1 :]
            value = gl * gl / (hl + reg_lambda)
            value = value + (g - gl) * (g - gl) / (h - hl + reg_lambda)
            value = value - g * g / (h + reg_lambda)
            gains_out[n, f : f + 1, :] = 0.5 * jnp.sum(value, axis=0, keepdims=True)

    @pl.when(k == kp)
    def _():
        for j in range(1, Z):
            z_copy(j).wait_send()

    for j in range(1, FEATS):
        side_copy(j).wait_send()

    def end_client(j, carry):
        codes_copy(j).wait_send()
        sums_copy(j).wait_send()
        return carry

    lax.fori_loop(1, CLIENTS, end_client, 0)

    def end_piece(t, carry):
        piece_sends(t, wait_send)
        return carry

    lax.fori_loop(0, 16, end_piece, 0)


def local(bin_codes, node_ids, margins, labels, split_feature, split_bin):
    vmem = pl.BlockSpec(memory_space=pltpu.VMEM)
    smem = pl.BlockSpec(memory_space=pltpu.SMEM)
    dma = pltpu.SemaphoreType.DMA
    return pl.pallas_call(
        kernel,
        out_shape=(
            jax.ShapeDtypeStruct((NODES, OWNED, BINS), F32),
            jax.ShapeDtypeStruct((2 * NODES, TARGETS), F32),
            jax.ShapeDtypeStruct((TARGETS, ROWS), F32),
        ),
        in_specs=[smem, smem, vmem, vmem, vmem, vmem],
        out_specs=(vmem, vmem, vmem),
        scratch_shapes=[
            pltpu.VMEM((CLIENTS, 3, 2, HALF), BF16),
            pltpu.VMEM((CLIENTS, 3, 2, HALF), BF16),
            pltpu.VMEM((CH, ROWS), BF16),
            pltpu.VMEM((2 * X * Y, 4, CH, QUARTER), BF16),
            pltpu.VMEM((FEATS, 2, HALF), BF16),
            pltpu.VMEM((CLIENTS, NODES, 128), F32),
            pltpu.VMEM((NODES * CH, OWNED * BINS), F32),
            dma((CLIENTS,)),
            dma((CLIENTS,)),
            dma((FEATS,)),
            dma((FEATS,)),
            dma((CLIENTS,)),
            dma((CLIENTS,)),
            dma((Z,)),
            dma((4,)),
            dma((80,)),
            dma((2 * X * Y,)),
        ],
        compiler_params=pltpu.CompilerParams(
            collective_id=0, has_side_effects=True, vmem_limit_bytes=60 << 20
        ),
        name="level",
    )(split_feature, split_bin, bin_codes, node_ids.reshape(1, ROWS), margins, labels)


def solution(mesh):
    in_specs = (P("feat", "client"), P("client"), P(None, "client"), P(None, "client"), P(), P())
    out_specs = (P(None, ("feat", "client"), None), P(), P(None, "client"))
    return jax.shard_map(local, mesh=mesh, in_specs=in_specs, out_specs=out_specs, check_vma=False)
```

```python
import jax
import jax.numpy as jnp
from jax import lax
from jax.experimental import pallas as pl
from jax.experimental.pallas import tpu as pltpu
from jax.sharding import PartitionSpec as P

F32 = jnp.float32
BF16 = jnp.bfloat16
MESH = pl.DeviceIdType.MESH
BINS = 256
NODES = 8
TARGETS = 16
CH = 2 * TARGETS
X, Y, Z = 4, 4, 8
CLIENTS = X * Z
FEATS = 2 * Y
ROWS = 1536
QUARTER = ROWS // Y
HALF = ROWS // 2
SLAB = 64
OWNED = 2
reg_lambda = 1.0
step_eta = 0.5
ORDER = (
    (0, 0), (1, 0), (3, 0), (0, 1), (0, 3), (1, 1), (3, 3), (1, 3), (3, 1),
    (2, 0), (0, 2), (2, 1), (2, 3), (1, 2), (3, 2), (2, 2),
)
AHEAD = 2
CONTRACT_LAST = (((1,), (1,)), ((), ()))


def split3(a):
    hi = a.astype(BF16)
    rest = a - hi.astype(F32)
    mid = rest.astype(BF16)
    low = (rest - mid.astype(F32)).astype(BF16)
    return hi, mid, low


def dot3(a, b):
    hi, mid, low = split3(a)
    out = jnp.dot(low, b, preferred_element_type=F32)
    out = out + jnp.dot(mid, b, preferred_element_type=F32)
    return out + jnp.dot(hi, b, preferred_element_type=F32)


def remote(src, dst, send, recv, client, feat):
    return pltpu.make_async_remote_copy(
        src_ref=src,
        dst_ref=dst,
        send_sem=send,
        recv_sem=recv,
        device_id=(client, feat),
        device_id_type=MESH,
    )


def kernel(
    feature_in,
    bin_in,
    codes_in,
    node_in,
    margins_in,
    labels_in,
    gains_out,
    leaf_out,
    margins_out,
    split_feature,
    split_bin,
    codes,
    node_ids,
    margins,
    labels,
    ls,
    msg,
    codes_all,
    stats,
    pieces,
    sides,
    child_ref,
    parts,
    sums,
    node_sums,
    acc,
    far,
    ss_codes,
    rs_codes,
    ss_side,
    rs_side,
    ss_sums,
    rs_sums,
    ss_node,
    rs_node,
    ss_z,
    rs_z,
    ss_piece,
    rs_piece,
):
    me = lax.axis_index("client")
    feat = lax.axis_index("feat")
    x = lax.div(me, Z)
    z = lax.rem(me, Z)
    y = lax.div(feat, 2)
    k = lax.rem(feat, 2)
    kp = lax.rem(z, 2)
    zz_own = lax.div(z, 2)

    barrier = pltpu.get_barrier_semaphore()

    for j in (4, 3, 5, 2, 6, 1, 7):
        pl.semaphore_signal(
            barrier, inc=1, device_id=(x * Z + lax.rem(z + j, Z), feat), device_id_type=MESH
        )
    for j in (2, 1, 3):
        pl.semaphore_signal(
            barrier, inc=1, device_id=((lax.rem(x + j, X)) * Z + z, feat), device_id_type=MESH
        )
    for j in range(1, FEATS):
        pl.semaphore_signal(
            barrier, inc=1, device_id=(me, lax.rem(feat + j, FEATS)), device_id_type=MESH
        )

    loads = [
        pltpu.make_async_copy(src, dst, ls.at[i])
        for i, (src, dst) in enumerate(
            (
                (margins_in, margins),
                (labels_in, labels),
                (node_in, node_ids),
                (codes_in, codes),
                (feature_in, split_feature),
                (bin_in, split_bin),
            )
        )
    ]
    for load in loads:
        load.start()
    for load in loads:
        load.wait()

    node = jnp.concatenate([node_ids[i : i + 1, :] for i in range(ROWS // 128)], axis=1)

    node_f = node.astype(F32)
    node_pair = jnp.concatenate([node_f[:, :HALF], node_f[:, HALF:]], axis=0).astype(BF16)

    def fill(q, carry):
        block = codes[pl.ds(pl.multiple_of(8 * q, 8), 8), :].astype(F32)
        for i in range(4):
            pair = block[OWNED * i : OWNED * (i + 1)].astype(BF16)
            msg[4 * q + i, 0] = pair[:, :HALF]
            msg[4 * q + i, 1] = pair[:, HALF:]
            msg[4 * q + i, 2] = node_pair
        return carry

    lax.fori_loop(0, CLIENTS // 4, fill, 0)

    probability = 1.0 / (1.0 + jnp.exp(-margins[...]))
    stats[0:TARGETS, :] = (probability - labels[...]).astype(BF16)
    stats[TARGETS:CH, :] = (probability * (1.0 - probability)).astype(BF16)

    side = jnp.zeros((1, ROWS), F32)
    for n in range(NODES):
        column = split_feature[n] - feat * SLAB
        held = jnp.where((column >= 0) & (column < SLAB), 1.0, 0.0)
        row = codes[pl.ds(jnp.clip(column, 0, SLAB - 1), 1), :]
        right = jnp.where((row > split_bin[n]) & (node == n), 1.0, 0.0)
        side = side + held * right
    sides[feat] = jnp.concatenate([side[:, :HALF], side[:, HALF:]], axis=0).astype(BF16)

    def piece_at(ra, rb, par):
        ax = ra * (1 - par) + rb * par
        ay = ra * par + rb * (1 - par)
        px = lax.rem(x + ax, X)
        quarter = lax.rem(y + ay, Y)
        return px, quarter, (quarter * X + px) * 2 + par

    first = piece_at(0, 0, k)[2]

    @pl.when(k == kp)
    def _():
        pieces[first, zz_own] = stats[:, pl.ds(pl.multiple_of(y * QUARTER, 128), QUARTER)]

    pl.semaphore_wait(barrier, Z - 1 + X - 1 + FEATS - 1)

    def z_copy(j):
        to = lax.rem(z + j, Z)
        return remote(
            pieces.at[first, zz_own],
            pieces.at[first, zz_own],
            ss_z.at[to],
            rs_z.at[zz_own],
            x * Z + to,
            feat,
        )

    @pl.when(k == kp)
    def _():
        for j in (4, 3, 5, 2, 6, 1, 7):
            z_copy(j).start()

    def codes_copy(dx, dz):
        to = lax.rem(x + dx, X) * Z + lax.rem(z + dz, Z)
        return remote(msg.at[to], codes_all.at[me], ss_codes, rs_codes.at[me], to, feat)

    for j in (4, 3, 5, 2, 6, 1, 7):
        codes_copy(0, j).start()
    for j in range(1, Z):
        pl.semaphore_signal(
            far, inc=1, device_id=(x * Z + lax.rem(z + j, Z), feat), device_id_type=MESH
        )

    def side_copy(j):
        to = lax.rem(feat + j, FEATS)
        return remote(sides.at[feat], sides.at[feat], ss_side, rs_side, me, to)

    for j in range(1, FEATS):
        side_copy(j).start()
    own_codes = pltpu.make_async_copy(msg.at[me], codes_all.at[me], rs_codes.at[me])
    own_codes.start()
    pl.semaphore_wait(far, Z - 1)

    def send_codes(dz, carry):
        for dx in (1, 3, 2):
            codes_copy(dx, dz).start()
        return carry

    lax.fori_loop(0, Z, send_codes, 0)

    def sums_copy(j):
        to = lax.rem(me + j, CLIENTS)
        return remote(sums.at[me], sums.at[me], ss_sums, rs_sums, to, feat)

    def node_copy(j):
        to = lax.rem(feat + j, FEATS)
        return remote(node_sums.at[feat], node_sums.at[feat], ss_node, rs_node, me, to)

    def many(ref, count, send, recv):
        return remote(ref.at[pl.ds(0, count)], ref.at[pl.ds(0, count)], send, recv, me, feat)

    def client_sums():
        many(sides, FEATS - 1, ss_side, rs_side).wait_recv()
        side_pair = sides[0].astype(F32)
        for j in range(1, FEATS):
            side_pair = side_pair + sides[j].astype(F32)
        side = jnp.concatenate([side_pair[0:1], side_pair[1:2]], axis=1)
        child = 2 * node + side.astype(jnp.int32)
        child_ref[...] = child
        node_iota = lax.broadcasted_iota(jnp.int32, (NODES, ROWS), 0)
        left_mask = jnp.where(2 * node_iota == child, 1.0, 0.0)
        node_mask = jnp.where(node_iota == node, 1.0, 0.0)
        mask = jnp.concatenate([left_mask, node_mask], axis=0).astype(BF16)
        part = lax.dot_general(mask, stats[...], CONTRACT_LAST, preferred_element_type=F32)
        parts[...] = jnp.concatenate([part, jnp.zeros((2 * NODES, 128 - CH), F32)], axis=1)
        sums[me] = jnp.concatenate(
            [
                parts[pl.ds(feat, 1), :CH],
                parts[pl.ds(NODES + feat, 1), :CH],
                jnp.zeros((1, 128 - 2 * CH), F32),
            ],
            axis=1,
        )

        def send_sums(j, carry):
            sums_copy(j).start()
            return carry

        lax.fori_loop(1, CLIENTS, send_sums, 0)

    def meet_nodes():
        many(sums, CLIENTS - 1, ss_sums, rs_sums).wait_recv()
        node_sums[feat] = jnp.sum(sums[...], axis=0)
        for j in range(1, FEATS):
            node_copy(j).start()

    def order(t):
        code = 0
        for i, (ra, rb) in enumerate(ORDER):
            code = code + jnp.where(t == i, 4 * ra + rb, 0)
        return lax.div(code, 4), lax.rem(code, 4)

    def along(da, db):
        ax = da * (1 - k) + db * k
        ay = da * k + db * (1 - k)
        return (lax.rem(x + ax, X)) * Z + z, (lax.rem(y + ay, Y)) * 2 + k

    def piece_copy(p, client, to_feat):
        return remote(pieces.at[p], pieces.at[p], ss_piece, rs_piece.at[p], client, to_feat)

    def piece_sends(ra, rb):
        p = piece_at(ra, rb, k)[2]
        piece_copy(p, me, y * 2 + (1 - k)).start()

        @pl.when((rb == 0) & (ra == 0))
        def _():
            for d in (1, 3):
                piece_copy(p, *along(d, 0)).start()

        @pl.when((rb == 0) & (ra == 1))
        def _():
            piece_copy(p, *along(3, 0)).start()

        @pl.when(rb == 0)
        def _():
            for d in (1, 3):
                piece_copy(p, *along(0, d)).start()

        @pl.when((rb == 3) & ((ra == 1) | (ra == 2)))
        def _():
            piece_copy(p, *along(0, 1)).start()

        @pl.when((rb == 1) & ((ra == 0) | (ra == 3)))
        def _():
            piece_copy(p, *along(0, 3)).start()

    def wait_piece(p):
        remote(
            pieces.at[p], pieces.at[p], ss_piece, rs_piece.at[p], me, y * 2 + (1 - k)
        ).wait_recv()

    for j in range(4):

        @pl.when(2 * j + k != z)
        def _():
            remote(
                pieces.at[first, j],
                pieces.at[first, j],
                ss_z.at[2 * j + k],
                rs_z.at[j],
                x * Z + 2 * j + k,
                feat,
            ).wait_recv()

    piece_sends(0, 0)

    def event(t):
        ra, rb = order(t)
        wait_piece(piece_at(ra, rb, k)[2])
        piece_sends(ra, rb)

    acc[...] = jnp.zeros_like(acc)

    def wait_codes(px, par):
        for j in range(4):
            frm = px * Z + 2 * j + par
            pltpu.make_async_copy(msg.at[frm], codes_all.at[frm], rs_codes.at[frm]).wait()

    def compute(steps):
        code_list = []
        node_list = []
        stat_list = []
        for ra, rb in steps:
            for which in range(2):
                par = k * (1 - which) + (1 - k) * which
                px, quarter, p = piece_at(ra, rb, par)

                @pl.when(((1 - par) * rb + par * ra) == 0)
                def _():
                    wait_codes(px, par)

                if which == 1:
                    wait_piece(p)
                half = lax.div(quarter, 2)
                lanes = pl.ds(pl.multiple_of(lax.rem(quarter, 2) * QUARTER, 128), QUARTER)
                for j in range(4):
                    frm = px * Z + 2 * j + par
                    code_list.append(codes_all[frm, half, :, lanes].astype(F32))
                    pair = codes_all[frm, 2, :, lanes].astype(F32)
                    node_list.append(jnp.where(half == 0, pair[0:1], pair[1:2]))
                    stat_list.append(pieces[p, j])
        code = jnp.concatenate(code_list, axis=1).astype(jnp.int32)
        nodes = jnp.concatenate(node_list, axis=1).astype(jnp.int32)
        stat = jnp.concatenate(stat_list, axis=1).astype(F32)
        width = code.shape[1]
        bin_iota = lax.broadcasted_iota(jnp.int32, (BINS, width), 0)
        onehot = jnp.concatenate(
            [jnp.where(code[f : f + 1] == bin_iota, 1.0, 0.0).astype(BF16) for f in range(OWNED)],
            axis=0,
        )
        spread = jnp.concatenate(
            [jnp.where(nodes == n, stat, 0.0).astype(BF16) for n in range(NODES)], axis=0
        )
        acc[...] += lax.dot_general(spread, onehot, CONTRACT_LAST, preferred_element_type=F32)

    compute([(0, 0)])
    client_sums()
    event(1)
    event(2)

    def step(t, carry):
        @pl.when(t < 7)
        def _():
            event(2 * t + 1)
            event(2 * t + 2)

        @pl.when(t == 7)
        def _():
            event(15)

        @pl.when(t == 5)
        def _():
            meet_nodes()

        compute([order(2 * t - 1), order(2 * t)])
        return carry

    lax.fori_loop(1, 8, step, 0)
    compute([order(15 + 0 * k)])

    many(node_sums, FEATS - 1, ss_node, rs_node).wait_recv()
    total = jnp.concatenate([node_sums[n] for n in range(NODES)], axis=0)
    left = total[:, :CH]
    whole = total[:, CH : 2 * CH]
    right = whole - left
    left_weight = -left[:, :TARGETS] / (left[:, TARGETS:] + reg_lambda)
    right_weight = -right[:, :TARGETS] / (right[:, TARGETS:] + reg_lambda)
    rows = []
    for n in range(NODES):
        rows.append(left_weight[n : n + 1])
        rows.append(right_weight[n : n + 1])
    weights = jnp.concatenate(rows, axis=0)
    leaf_out[...] = weights
    columns = jnp.concatenate([weights, jnp.zeros((2 * NODES, 128 - TARGETS), F32)], axis=1).T
    child_iota = lax.broadcasted_iota(jnp.int32, (2 * NODES, ROWS), 0)
    child_mask = jnp.where(child_iota == child_ref[...], 1.0, 0.0).astype(BF16)
    lookup = dot3(columns[:TARGETS, :], child_mask)
    margins_out[...] = margins[...] + step_eta * lookup

    row_bin = lax.broadcasted_iota(jnp.int32, (BINS, BINS), 0)
    col_bin = lax.broadcasted_iota(jnp.int32, (BINS, BINS), 1)
    upto = jnp.where(row_bin <= col_bin, 1.0, 0.0).astype(BF16)
    for f in range(OWNED):
        prefix = dot3(acc[:, f * BINS : (f + 1) * BINS], upto)
        for n in range(NODES):
            gl = prefix[n * CH : n * CH + TARGETS]
            hl = prefix[n * CH + TARGETS : (n + 1) * CH]
            g = gl[:, BINS - 1 :]
            h = hl[:, BINS - 1 :]
            value = gl * gl / (hl + reg_lambda)
            value = value + (g - gl) * (g - gl) / (h - hl + reg_lambda)
            value = value - g * g / (h + reg_lambda)
            gains_out[n, f : f + 1, :] = 0.5 * jnp.sum(value, axis=0, keepdims=True)

    @pl.when(k == kp)
    def _():
        for j in range(1, Z):
            z_copy(j).wait_send()

    many(sides, FEATS - 1, ss_side, rs_side).wait_send()
    many(node_sums, FEATS - 1, ss_node, rs_node).wait_send()
    many(sums, CLIENTS - 1, ss_sums, rs_sums).wait_send()
    many(msg, CLIENTS - 1, ss_codes, rs_codes.at[0]).wait_send()
    many(pieces, 2 * X * Y - 1, ss_piece, rs_piece.at[0]).wait_send()


def local(bin_codes, node_ids, margins, labels, split_feature, split_bin):
    vmem = pl.BlockSpec(memory_space=pltpu.VMEM)
    hbm = pl.BlockSpec(memory_space=pltpu.HBM)
    dma = pltpu.SemaphoreType.DMA
    return pl.pallas_call(
        kernel,
        out_shape=(
            jax.ShapeDtypeStruct((NODES, OWNED, BINS), F32),
            jax.ShapeDtypeStruct((2 * NODES, TARGETS), F32),
            jax.ShapeDtypeStruct((TARGETS, ROWS), F32),
        ),
        in_specs=[hbm] * 6,
        out_specs=(vmem, vmem, vmem),
        scratch_shapes=[
            pltpu.SMEM((NODES,), jnp.int32),
            pltpu.SMEM((NODES,), jnp.int32),
            pltpu.VMEM((SLAB, ROWS), jnp.int32),
            pltpu.VMEM((ROWS // 128, 128), jnp.int32),
            pltpu.VMEM((TARGETS, ROWS), F32),
            pltpu.VMEM((TARGETS, ROWS), F32),
            dma((6,)),
            pltpu.VMEM((CLIENTS, 3, 2, HALF), BF16),
            pltpu.VMEM((CLIENTS, 3, 2, HALF), BF16),
            pltpu.VMEM((CH, ROWS), BF16),
            pltpu.VMEM((2 * X * Y, 4, CH, QUARTER), BF16),
            pltpu.VMEM((FEATS, 2, HALF), BF16),
            pltpu.VMEM((1, ROWS), jnp.int32),
            pltpu.VMEM((2 * NODES, 128), F32),
            pltpu.VMEM((CLIENTS, 1, 128), F32),
            pltpu.VMEM((FEATS, 1, 128), F32),
            pltpu.VMEM((NODES * CH, OWNED * BINS), F32),
            pltpu.SemaphoreType.REGULAR,
            dma,
            dma((CLIENTS,)),
            dma,
            dma,
            dma,
            dma,
            dma,
            dma,
            dma((Z,)),
            dma((4,)),
            dma,
            dma((2 * X * Y,)),
        ],
        compiler_params=pltpu.CompilerParams(
            collective_id=0, has_side_effects=True, vmem_limit_bytes=36 << 20
        ),
        name="level",
    )(*[pltpu.with_memory_space_constraint(a, pltpu.HBM) for a in (split_feature, split_bin, bin_codes, node_ids.reshape(ROWS // 128, 128), margins, labels)])


def solution(mesh):
    in_specs = (P("feat", "client"), P("client"), P(None, "client"), P(None, "client"), P(), P())
    out_specs = (P(None, ("feat", "client"), None), P(), P(None, "client"))
    return jax.shard_map(local, mesh=mesh, in_specs=in_specs, out_specs=out_specs, check_vma=False)
```

```python
import jax
import jax.numpy as jnp
from jax import lax
from jax.experimental import pallas as pl
from jax.experimental.pallas import tpu as pltpu
from jax.sharding import PartitionSpec as P

F32 = jnp.float32
BF16 = jnp.bfloat16
MESH = pl.DeviceIdType.MESH
BINS = 256
NODES = 8
TARGETS = 16
CH = 2 * TARGETS
X, Y, Z = 4, 4, 8
CLIENTS = X * Z
FEATS = 2 * Y
ROWS = 1536
QUARTER = ROWS // Y
HALF = ROWS // 2
SLAB = 64
OWNED = 2
reg_lambda = 1.0
step_eta = 0.5
PLAN = (
    ("add", 0, 0), ("sums",), ("near", 0, 1), ("near", 0, 3), ("near", 1, 0), ("near", 3, 0), ("codes",), ("add", 0, 1, 0, 3),
    ("take", 2, 0), ("add", 1, 0, 3, 0), ("take", 1, 1),
    ("take", 1, 3), ("take", 3, 1), ("take", 3, 3), ("take", 0, 2), ("add", 0, 2, 2, 0),
    ("add", 1, 1, 1, 3), ("take", 2, 1), ("take", 2, 3), ("add", 3, 1, 3, 3), ("take", 1, 2),
    ("take", 3, 2), ("meet",), ("add", 1, 2, 3, 2), ("take", 2, 2), ("add", 2, 1, 2, 3),
    ("add", 2, 2),
)
CONTRACT_LAST = (((1,), (1,)), ((), ()))


def split3(a):
    hi = a.astype(BF16)
    rest = a - hi.astype(F32)
    mid = rest.astype(BF16)
    low = (rest - mid.astype(F32)).astype(BF16)
    return hi, mid, low


def dot3(a, b):
    hi, mid, low = split3(a)
    out = jnp.dot(low, b, preferred_element_type=F32)
    out = out + jnp.dot(mid, b, preferred_element_type=F32)
    return out + jnp.dot(hi, b, preferred_element_type=F32)


def remote(src, dst, send, recv, client, feat):
    return pltpu.make_async_remote_copy(
        src_ref=src,
        dst_ref=dst,
        send_sem=send,
        recv_sem=recv,
        device_id=(client, feat),
        device_id_type=MESH,
    )


def kernel(
    feature_in,
    bin_in,
    codes_in,
    node_in,
    margins_in,
    labels_in,
    gains_out,
    leaf_out,
    margins_out,
    split_feature,
    split_bin,
    codes,
    node_ids,
    margins,
    labels,
    ls,
    msg,
    codes_all,
    stats,
    pieces,
    sides,
    child_ref,
    parts,
    sums,
    node_sums,
    acc,
    far,
    ss_codes,
    rs_codes,
    ss_side,
    rs_side,
    ss_sums,
    rs_sums,
    ss_node,
    rs_node,
    ss_z,
    rs_z,
    ss_piece,
    rs_piece,
):
    me = lax.axis_index("client")
    feat = lax.axis_index("feat")
    x = lax.div(me, Z)
    z = lax.rem(me, Z)
    y = lax.div(feat, 2)
    k = lax.rem(feat, 2)
    kp = lax.rem(z, 2)
    zz_own = lax.div(z, 2)

    barrier = pltpu.get_barrier_semaphore()

    for j in (4, 3, 5, 2, 6, 1, 7):
        pl.semaphore_signal(
            barrier, inc=1, device_id=(x * Z + lax.rem(z + j, Z), feat), device_id_type=MESH
        )
    for j in (2, 1, 3):
        pl.semaphore_signal(
            barrier, inc=1, device_id=((lax.rem(x + j, X)) * Z + z, feat), device_id_type=MESH
        )
    for j in range(1, FEATS):
        pl.semaphore_signal(
            barrier, inc=1, device_id=(me, lax.rem(feat + j, FEATS)), device_id_type=MESH
        )

    loads = [
        pltpu.make_async_copy(src, dst, ls.at[i])
        for i, (src, dst) in enumerate(
            (
                (margins_in, margins),
                (labels_in, labels),
                (node_in, node_ids),
                (codes_in, codes),
                (feature_in, split_feature),
                (bin_in, split_bin),
            )
        )
    ]
    for load in loads:
        load.start()
    for load in loads[:2]:
        load.wait()
    probability = 1.0 / (1.0 + jnp.exp(-margins[...]))
    stats[0:TARGETS, :] = (probability - labels[...]).astype(BF16)
    stats[TARGETS:CH, :] = (probability * (1.0 - probability)).astype(BF16)

    def piece_at(dx, dy, par):
        px = lax.rem(x + dx, X)
        quarter = lax.rem(y + dy, Y)
        return px, quarter, (quarter * X + px) * 2 + par

    first = piece_at(0, 0, k)[2]

    @pl.when(k == kp)
    def _():
        pieces[first, zz_own] = stats[:, pl.ds(pl.multiple_of(y * QUARTER, 128), QUARTER)]

    pl.semaphore_wait(barrier, Z - 1 + X - 1 + FEATS - 1)

    def z_copy(j):
        to = lax.rem(z + j, Z)
        return remote(
            pieces.at[first, zz_own],
            pieces.at[first, zz_own],
            ss_z.at[to],
            rs_z.at[zz_own],
            x * Z + to,
            feat,
        )

    @pl.when(k == kp)
    def _():
        for j in (4, 3, 5, 2, 6, 1, 7):
            z_copy(j).start()

    for load in loads[2:]:
        load.wait()
    node = jnp.concatenate([node_ids[i : i + 1, :] for i in range(ROWS // 128)], axis=1)

    node_f = node.astype(F32)
    node_pair = jnp.concatenate([node_f[:, :HALF], node_f[:, HALF:]], axis=0).astype(BF16)

    def fill(q, carry):
        block = codes[pl.ds(pl.multiple_of(8 * q, 8), 8), :].astype(F32)
        for i in range(4):
            pair = block[OWNED * i : OWNED * (i + 1)].astype(BF16)
            msg[4 * q + i, 0] = pair[:, :HALF]
            msg[4 * q + i, 1] = pair[:, HALF:]
            msg[4 * q + i, 2] = node_pair
        return carry

    lax.fori_loop(0, CLIENTS // 4, fill, 0)

    side = jnp.zeros((1, ROWS), F32)
    for n in range(NODES):
        column = split_feature[n] - feat * SLAB
        held = jnp.where((column >= 0) & (column < SLAB), 1.0, 0.0)
        row = codes[pl.ds(jnp.clip(column, 0, SLAB - 1), 1), :]
        right = jnp.where((row > split_bin[n]) & (node == n), 1.0, 0.0)
        side = side + held * right
    sides[feat] = jnp.concatenate([side[:, :HALF], side[:, HALF:]], axis=0).astype(BF16)

    def codes_copy(dx, dz):
        to = lax.rem(x + dx, X) * Z + lax.rem(z + dz, Z)
        return remote(msg.at[to], codes_all.at[me], ss_codes, rs_codes.at[me], to, feat)

    for j in (4, 3, 5, 2, 6, 1, 7):
        codes_copy(0, j).start()
    for j in range(1, Z):
        pl.semaphore_signal(
            far, inc=1, device_id=(x * Z + lax.rem(z + j, Z), feat), device_id_type=MESH
        )

    def side_copy(j):
        to = lax.rem(feat + j, FEATS)
        return remote(sides.at[feat], sides.at[feat], ss_side, rs_side, me, to)

    for j in range(1, FEATS):
        side_copy(j).start()
    own_codes = pltpu.make_async_copy(msg.at[me], codes_all.at[me], rs_codes.at[me])
    own_codes.start()
    def along(da, db):
        ax = da * (1 - k) + db * k
        ay = da * k + db * (1 - k)
        return (lax.rem(x + ax, X)) * Z + z, (lax.rem(y + ay, Y)) * 2 + k

    def piece_copy(p, client, to_feat):
        return remote(pieces.at[p], pieces.at[p], ss_piece, rs_piece.at[p], client, to_feat)

    def own_piece(ra, rb):
        return piece_at(ra * (1 - k) + rb * k, ra * k + rb * (1 - k), k)[2]

    def piece_sends(ra, rb):
        p = own_piece(ra, rb)
        to = []
        if rb == 0 and ra == 0:
            to += [(1, 0), (3, 0), (2, 0)]
        if rb == 0:
            to += [(0, 1), (0, 3)]
        if rb == 3 and ra in (1, 2):
            to += [(0, 1)]
        if rb == 1 and ra in (0, 3):
            to += [(0, 3)]
        for da, db in to:
            piece_copy(p, *along(da, db)).start()
        piece_copy(p, me, y * 2 + (1 - k)).start()

    def wait_piece(p):
        remote(
            pieces.at[p], pieces.at[p], ss_piece, rs_piece.at[p], me, y * 2 + (1 - k)
        ).wait_recv()

    for j in range(4):

        @pl.when(2 * j + k != z)
        def _():
            remote(
                pieces.at[first, j],
                pieces.at[first, j],
                ss_z.at[2 * j + k],
                rs_z.at[j],
                x * Z + 2 * j + k,
                feat,
            ).wait_recv()

    piece_sends(0, 0)
    pl.semaphore_wait(far, Z - 1)

    for dz in (0, 4, 3, 5, 2, 6, 1, 7):
        for dx in (1, 3):
            codes_copy(dx, dz).start()

    def sums_copy(j):
        to = lax.rem(me + j, CLIENTS)
        return remote(sums.at[me], sums.at[me], ss_sums, rs_sums, to, feat)

    def node_copy(j):
        to = lax.rem(feat + j, FEATS)
        return remote(node_sums.at[feat], node_sums.at[feat], ss_node, rs_node, me, to)

    def many(ref, count, send, recv):
        return remote(ref.at[pl.ds(0, count)], ref.at[pl.ds(0, count)], send, recv, me, feat)

    def client_sums():
        many(sides, FEATS - 1, ss_side, rs_side).wait_recv()
        side_pair = sides[0].astype(F32)
        for j in range(1, FEATS):
            side_pair = side_pair + sides[j].astype(F32)
        side = jnp.concatenate([side_pair[0:1], side_pair[1:2]], axis=1)
        child = 2 * node + side.astype(jnp.int32)
        child_ref[...] = child
        node_iota = lax.broadcasted_iota(jnp.int32, (NODES, ROWS), 0)
        left_mask = jnp.where(2 * node_iota == child, 1.0, 0.0)
        node_mask = jnp.where(node_iota == node, 1.0, 0.0)
        mask = jnp.concatenate([left_mask, node_mask], axis=0).astype(BF16)
        part = lax.dot_general(mask, stats[...], CONTRACT_LAST, preferred_element_type=F32)
        parts[...] = jnp.concatenate([part, jnp.zeros((2 * NODES, 128 - CH), F32)], axis=1)
        sums[me] = jnp.concatenate(
            [
                parts[pl.ds(feat, 1), :CH],
                parts[pl.ds(NODES + feat, 1), :CH],
                jnp.zeros((1, 128 - 2 * CH), F32),
            ],
            axis=1,
        )

        for j in range(1, CLIENTS):
            sums_copy(j).start()

    def meet_nodes():
        many(sums, CLIENTS - 1, ss_sums, rs_sums).wait_recv()
        node_sums[feat] = jnp.sum(sums[...], axis=0)
        for j in range(1, FEATS):
            node_copy(j).start()

    def event(ra, rb):
        wait_piece(own_piece(ra, rb))
        piece_sends(ra, rb)

    acc[...] = jnp.zeros_like(acc)

    def wait_codes(px, par):
        for j in range(4):
            frm = px * Z + 2 * j + par
            pltpu.make_async_copy(msg.at[frm], codes_all.at[frm], rs_codes.at[frm]).wait()

    def compute(steps):
        code_list = []
        node_list = []
        stat_list = []
        for dx, dy in steps:
            for which in range(2):
                par = k * (1 - which) + (1 - k) * which
                px, quarter, p = piece_at(dx, dy, par)
                if dy == 0:
                    wait_codes(px, par)
                if which == 1:
                    wait_piece(p)
                half = lax.div(quarter, 2)
                lanes = pl.ds(pl.multiple_of(lax.rem(quarter, 2) * QUARTER, 128), QUARTER)
                for j in range(4):
                    frm = px * Z + 2 * j + par
                    code_list.append(codes_all[frm, half, :, lanes].astype(F32))
                    pair = codes_all[frm, 2, :, lanes].astype(F32)
                    node_list.append(jnp.where(half == 0, pair[0:1], pair[1:2]))
                    stat_list.append(pieces[p, j])
        code = jnp.concatenate(code_list, axis=1).astype(jnp.int32)
        nodes = jnp.concatenate(node_list, axis=1).astype(jnp.int32)
        stat = jnp.concatenate(stat_list, axis=1).astype(F32)
        width = code.shape[1]
        bin_iota = lax.broadcasted_iota(jnp.int32, (BINS, width), 0)
        onehot = jnp.concatenate(
            [jnp.where(code[f : f + 1] == bin_iota, 1.0, 0.0).astype(BF16) for f in range(OWNED)],
            axis=0,
        )
        spread = jnp.concatenate(
            [jnp.where(nodes == n, stat, 0.0).astype(BF16) for n in range(NODES)], axis=0
        )
        acc[...] += lax.dot_general(spread, onehot, CONTRACT_LAST, preferred_element_type=F32)

    for what, *at in PLAN:
        if what == "sums":
            client_sums()
        elif what == "near":
            dx, dy = at
            wait_piece(piece_at(dx, dy, k)[2])
            for core in range(2):

                @pl.when(k == core)
                def _():
                    piece_sends(*((dx, dy) if core == 0 else (dy, dx)))

        elif what == "codes":
            for dz in (0, 4, 3, 5, 2, 6, 1, 7):
                codes_copy(2, dz).start()
        elif what == "meet":
            meet_nodes()
        elif what == "take":
            event(*at)
        else:
            compute(list(zip(at[::2], at[1::2])))

    many(node_sums, FEATS - 1, ss_node, rs_node).wait_recv()
    total = jnp.concatenate([node_sums[n] for n in range(NODES)], axis=0)
    left = total[:, :CH]
    whole = total[:, CH : 2 * CH]
    right = whole - left
    left_weight = -left[:, :TARGETS] / (left[:, TARGETS:] + reg_lambda)
    right_weight = -right[:, :TARGETS] / (right[:, TARGETS:] + reg_lambda)
    rows = []
    for n in range(NODES):
        rows.append(left_weight[n : n + 1])
        rows.append(right_weight[n : n + 1])
    weights = jnp.concatenate(rows, axis=0)
    leaf_out[...] = weights
    columns = jnp.concatenate([weights, jnp.zeros((2 * NODES, 128 - TARGETS), F32)], axis=1).T
    child_iota = lax.broadcasted_iota(jnp.int32, (2 * NODES, ROWS), 0)
    child_mask = jnp.where(child_iota == child_ref[...], 1.0, 0.0).astype(BF16)
    lookup = dot3(columns[:TARGETS, :], child_mask)
    margins_out[...] = margins[...] + step_eta * lookup

    row_bin = lax.broadcasted_iota(jnp.int32, (BINS, BINS), 0)
    col_bin = lax.broadcasted_iota(jnp.int32, (BINS, BINS), 1)
    upto = jnp.where(row_bin <= col_bin, 1.0, 0.0).astype(BF16)
    for f in range(OWNED):
        prefix = dot3(acc[:, f * BINS : (f + 1) * BINS], upto)
        for n in range(NODES):
            gl = prefix[n * CH : n * CH + TARGETS]
            hl = prefix[n * CH + TARGETS : (n + 1) * CH]
            g = gl[:, BINS - 1 :]
            h = hl[:, BINS - 1 :]
            value = gl * gl / (hl + reg_lambda)
            value = value + (g - gl) * (g - gl) / (h - hl + reg_lambda)
            value = value - g * g / (h + reg_lambda)
            gains_out[n, f : f + 1, :] = 0.5 * jnp.sum(value, axis=0, keepdims=True)

    @pl.when(k == kp)
    def _():
        for j in range(1, Z):
            z_copy(j).wait_send()

    many(sides, FEATS - 1, ss_side, rs_side).wait_send()
    many(node_sums, FEATS - 1, ss_node, rs_node).wait_send()
    many(sums, CLIENTS - 1, ss_sums, rs_sums).wait_send()
    many(msg, CLIENTS - 1, ss_codes, rs_codes.at[0]).wait_send()
    many(pieces, 2 * X * Y - 1, ss_piece, rs_piece.at[0]).wait_send()


def local(bin_codes, node_ids, margins, labels, split_feature, split_bin):
    vmem = pl.BlockSpec(memory_space=pltpu.VMEM)
    hbm = pl.BlockSpec(memory_space=pltpu.HBM)
    dma = pltpu.SemaphoreType.DMA
    return pl.pallas_call(
        kernel,
        out_shape=(
            jax.ShapeDtypeStruct((NODES, OWNED, BINS), F32),
            jax.ShapeDtypeStruct((2 * NODES, TARGETS), F32),
            jax.ShapeDtypeStruct((TARGETS, ROWS), F32),
        ),
        in_specs=[hbm] * 6,
        out_specs=(vmem, vmem, vmem),
        scratch_shapes=[
            pltpu.SMEM((NODES,), jnp.int32),
            pltpu.SMEM((NODES,), jnp.int32),
            pltpu.VMEM((SLAB, ROWS), jnp.int32),
            pltpu.VMEM((ROWS // 128, 128), jnp.int32),
            pltpu.VMEM((TARGETS, ROWS), F32),
            pltpu.VMEM((TARGETS, ROWS), F32),
            dma((6,)),
            pltpu.VMEM((CLIENTS, 3, 2, HALF), BF16),
            pltpu.VMEM((CLIENTS, 3, 2, HALF), BF16),
            pltpu.VMEM((CH, ROWS), BF16),
            pltpu.VMEM((2 * X * Y, 4, CH, QUARTER), BF16),
            pltpu.VMEM((FEATS, 2, HALF), BF16),
            pltpu.VMEM((1, ROWS), jnp.int32),
            pltpu.VMEM((2 * NODES, 128), F32),
            pltpu.VMEM((CLIENTS, 1, 128), F32),
            pltpu.VMEM((FEATS, 1, 128), F32),
            pltpu.VMEM((NODES * CH, OWNED * BINS), F32),
            pltpu.SemaphoreType.REGULAR,
            dma,
            dma((CLIENTS,)),
            dma,
            dma,
            dma,
            dma,
            dma,
            dma,
            dma((Z,)),
            dma((4,)),
            dma,
            dma((2 * X * Y,)),
        ],
        compiler_params=pltpu.CompilerParams(
            collective_id=0, has_side_effects=True, vmem_limit_bytes=36 << 20
        ),
        name="level",
    )(*[pltpu.with_memory_space_constraint(a, pltpu.HBM) for a in (split_feature, split_bin, bin_codes, node_ids.reshape(ROWS // 128, 128), margins, labels)])


def solution(mesh):
    in_specs = (P("feat", "client"), P("client"), P(None, "client"), P(None, "client"), P(), P())
    out_specs = (P(None, ("feat", "client"), None), P(), P(None, "client"))
    return jax.shard_map(local, mesh=mesh, in_specs=in_specs, out_specs=out_specs, check_vma=False)
```

```python
import jax
import jax.numpy as jnp
from jax import lax
from jax.experimental import pallas as pl
from jax.experimental.pallas import tpu as pltpu
from jax.sharding import PartitionSpec as P

F32 = jnp.float32
BF16 = jnp.bfloat16
MESH = pl.DeviceIdType.MESH
BINS = 256
NODES = 8
TARGETS = 16
CH = 2 * TARGETS
X, Y, Z = 4, 4, 8
CLIENTS = X * Z
FEATS = 2 * Y
ROWS = 1536
QUARTER = ROWS // Y
HALF = ROWS // 2
SLAB = 64
OWNED = 2
reg_lambda = 1.0
step_eta = 0.5
PLAN = (
    ("add", 0, 0), ("sums",), ("near", 0, 1), ("near", 0, 3), ("near", 1, 0), ("near", 3, 0),
    ("codes",), ("add", 0, 1, 0, 3), ("add", 1, 0, 3, 0), ("take", 2, 0), ("take", 1, 1), ("take", 1, 3),
    ("take", 3, 1), ("take", 3, 3), ("add", 1, 1, 1, 3), ("take", 0, 2), ("add", 3, 1, 3, 3),
    ("take", 2, 1), ("take", 2, 3), ("add", 0, 2, 2, 0), ("take", 1, 2), ("take", 3, 2),
    ("meet",), ("add", 1, 2, 3, 2), ("take", 2, 2), ("add", 2, 1, 2, 3), ("add", 2, 2),
)
CONTRACT_LAST = (((1,), (1,)), ((), ()))


def split3(a):
    hi = a.astype(BF16)
    rest = a - hi.astype(F32)
    mid = rest.astype(BF16)
    low = (rest - mid.astype(F32)).astype(BF16)
    return hi, mid, low


def dot3(a, b):
    hi, mid, low = split3(a)
    out = jnp.dot(low, b, preferred_element_type=F32)
    out = out + jnp.dot(mid, b, preferred_element_type=F32)
    return out + jnp.dot(hi, b, preferred_element_type=F32)


def remote(src, dst, send, recv, client, feat):
    return pltpu.make_async_remote_copy(
        src_ref=src,
        dst_ref=dst,
        send_sem=send,
        recv_sem=recv,
        device_id=(client, feat),
        device_id_type=MESH,
    )


def kernel(
    feature_in,
    bin_in,
    codes_in,
    node_in,
    margins_in,
    labels_in,
    gains_out,
    leaf_out,
    margins_out,
    split_feature,
    split_bin,
    codes,
    node_ids,
    margins,
    labels,
    ls,
    msg,
    codes_all,
    stats,
    pieces,
    sides,
    child_ref,
    parts,
    sums,
    node_sums,
    acc,
    far,
    ss_codes,
    rs_codes,
    ss_side,
    rs_side,
    ss_sums,
    rs_sums,
    ss_node,
    rs_node,
    ss_z,
    rs_z,
    ss_piece,
    rs_piece,
):
    me = lax.axis_index("client")
    feat = lax.axis_index("feat")
    x = lax.div(me, Z)
    z = lax.rem(me, Z)
    y = lax.div(feat, 2)
    k = lax.rem(feat, 2)
    kp = lax.rem(z, 2)
    zz_own = lax.div(z, 2)

    barrier = pltpu.get_barrier_semaphore()

    for j in (4, 3, 5, 2, 6, 1, 7):
        pl.semaphore_signal(
            barrier, inc=1, device_id=(x * Z + lax.rem(z + j, Z), feat), device_id_type=MESH
        )
    for j in (2, 1, 3):
        pl.semaphore_signal(
            barrier, inc=1, device_id=((lax.rem(x + j, X)) * Z + z, feat), device_id_type=MESH
        )
    for j in range(1, FEATS):
        pl.semaphore_signal(
            barrier, inc=1, device_id=(me, lax.rem(feat + j, FEATS)), device_id_type=MESH
        )

    loads = [
        pltpu.make_async_copy(src, dst, ls.at[i])
        for i, (src, dst) in enumerate(
            (
                (margins_in, margins),
                (labels_in, labels),
                (node_in, node_ids),
                (codes_in, codes),
                (feature_in, split_feature),
                (bin_in, split_bin),
            )
        )
    ]
    for load in loads:
        load.start()
    for load in loads[:2]:
        load.wait()
    probability = 1.0 / (1.0 + jnp.exp(-margins[...]))
    stats[0:TARGETS, :] = (probability - labels[...]).astype(BF16)
    stats[TARGETS:CH, :] = (probability * (1.0 - probability)).astype(BF16)

    def piece_at(dx, dy, par):
        px = lax.rem(x + dx, X)
        quarter = lax.rem(y + dy, Y)
        return px, quarter, (quarter * X + px) * 2 + par

    first = piece_at(0, 0, k)[2]

    @pl.when(k == kp)
    def _():
        pieces[first, zz_own] = stats[:, pl.ds(pl.multiple_of(y * QUARTER, 128), QUARTER)]

    pl.semaphore_wait(barrier, Z - 1 + X - 1 + FEATS - 1)

    def z_copy(j):
        to = lax.rem(z + j, Z)
        return remote(
            pieces.at[first, zz_own],
            pieces.at[first, zz_own],
            ss_z.at[to],
            rs_z.at[zz_own],
            x * Z + to,
            feat,
        )

    @pl.when(k == kp)
    def _():
        for j in (4, 3, 5, 2, 6, 1, 7):
            z_copy(j).start()

    for load in loads[2:]:
        load.wait()
    node = jnp.concatenate([node_ids[i : i + 1, :] for i in range(ROWS // 128)], axis=1)

    node_f = node.astype(F32)
    node_pair = jnp.concatenate([node_f[:, :HALF], node_f[:, HALF:]], axis=0).astype(BF16)

    def fill(q, carry):
        block = codes[pl.ds(pl.multiple_of(8 * q, 8), 8), :].astype(F32)
        for i in range(4):
            pair = block[OWNED * i : OWNED * (i + 1)].astype(BF16)
            msg[4 * q + i, 0] = pair[:, :HALF]
            msg[4 * q + i, 1] = pair[:, HALF:]
            msg[4 * q + i, 2] = node_pair
        return carry

    lax.fori_loop(0, CLIENTS // 4, fill, 0)

    side = jnp.zeros((1, ROWS), F32)
    for n in range(NODES):
        column = split_feature[n] - feat * SLAB
        held = jnp.where((column >= 0) & (column < SLAB), 1.0, 0.0)
        row = codes[pl.ds(jnp.clip(column, 0, SLAB - 1), 1), :]
        right = jnp.where((row > split_bin[n]) & (node == n), 1.0, 0.0)
        side = side + held * right
    sides[feat] = jnp.concatenate([side[:, :HALF], side[:, HALF:]], axis=0).astype(BF16)

    def codes_copy(dx, dz):
        to = lax.rem(x + dx, X) * Z + lax.rem(z + dz, Z)
        return remote(msg.at[to], codes_all.at[me], ss_codes, rs_codes.at[me], to, feat)

    for j in (4, 3, 5, 2, 6, 1, 7):
        codes_copy(0, j).start()
    for j in range(1, Z):
        pl.semaphore_signal(
            far, inc=1, device_id=(x * Z + lax.rem(z + j, Z), feat), device_id_type=MESH
        )

    def side_copy(j):
        to = lax.rem(feat + j, FEATS)
        return remote(sides.at[feat], sides.at[feat], ss_side, rs_side, me, to)

    for j in range(1, FEATS):
        side_copy(j).start()
    own_codes = pltpu.make_async_copy(msg.at[me], codes_all.at[me], rs_codes.at[me])
    own_codes.start()
    def along(da, db):
        ax = da * (1 - k) + db * k
        ay = da * k + db * (1 - k)
        return (lax.rem(x + ax, X)) * Z + z, (lax.rem(y + ay, Y)) * 2 + k

    def piece_copy(p, client, to_feat):
        return remote(pieces.at[p], pieces.at[p], ss_piece, rs_piece.at[p], client, to_feat)

    def own_piece(ra, rb):
        return piece_at(ra * (1 - k) + rb * k, ra * k + rb * (1 - k), k)[2]

    def piece_sends(ra, rb):
        p = own_piece(ra, rb)
        to = []
        if rb == 0 and ra == 0:
            to += [(1, 0), (3, 0), (2, 0)]
        if rb == 0:
            to += [(0, 1), (0, 3)]
        if rb == 3 and ra in (1, 2):
            to += [(0, 1)]
        if rb == 1 and ra in (0, 3):
            to += [(0, 3)]
        for da, db in to:
            piece_copy(p, *along(da, db)).start()
        piece_copy(p, me, y * 2 + (1 - k)).start()

    def wait_piece(p):
        remote(
            pieces.at[p], pieces.at[p], ss_piece, rs_piece.at[p], me, y * 2 + (1 - k)
        ).wait_recv()

    for j in range(4):

        @pl.when(2 * j + k != z)
        def _():
            remote(
                pieces.at[first, j],
                pieces.at[first, j],
                ss_z.at[2 * j + k],
                rs_z.at[j],
                x * Z + 2 * j + k,
                feat,
            ).wait_recv()

    piece_sends(0, 0)
    pl.semaphore_wait(far, Z - 1)

    for dz in (0, 4, 3, 5, 2, 6, 1, 7):
        for dx in (1, 3):
            codes_copy(dx, dz).start()

    def sums_copy(j):
        to = lax.rem(me + j, CLIENTS)
        return remote(sums.at[me], sums.at[me], ss_sums, rs_sums, to, feat)

    def node_copy(j):
        to = lax.rem(feat + j, FEATS)
        return remote(node_sums.at[feat], node_sums.at[feat], ss_node, rs_node, me, to)

    def many(ref, count, send, recv):
        return remote(ref.at[pl.ds(0, count)], ref.at[pl.ds(0, count)], send, recv, me, feat)

    def client_sums():
        many(sides, FEATS - 1, ss_side, rs_side).wait_recv()
        side_pair = sides[0].astype(F32)
        for j in range(1, FEATS):
            side_pair = side_pair + sides[j].astype(F32)
        side = jnp.concatenate([side_pair[0:1], side_pair[1:2]], axis=1)
        child = 2 * node + side.astype(jnp.int32)
        child_ref[...] = child
        node_iota = lax.broadcasted_iota(jnp.int32, (NODES, ROWS), 0)
        left_mask = jnp.where(2 * node_iota == child, 1.0, 0.0)
        node_mask = jnp.where(node_iota == node, 1.0, 0.0)
        mask = jnp.concatenate([left_mask, node_mask], axis=0).astype(BF16)
        part = lax.dot_general(mask, stats[...], CONTRACT_LAST, preferred_element_type=F32)
        parts[...] = jnp.concatenate([part, jnp.zeros((2 * NODES, 128 - CH), F32)], axis=1)
        sums[me] = jnp.concatenate(
            [
                parts[pl.ds(feat, 1), :CH],
                parts[pl.ds(NODES + feat, 1), :CH],
                jnp.zeros((1, 128 - 2 * CH), F32),
            ],
            axis=1,
        )

        for j in range(1, CLIENTS):
            sums_copy(j).start()

    def meet_nodes():
        many(sums, CLIENTS - 1, ss_sums, rs_sums).wait_recv()
        node_sums[feat] = jnp.sum(sums[...], axis=0)
        for j in range(1, FEATS):
            node_copy(j).start()

    def event(ra, rb):
        wait_piece(own_piece(ra, rb))
        piece_sends(ra, rb)

    acc[...] = jnp.zeros_like(acc)

    def wait_codes(px, par):
        for j in range(4):
            frm = px * Z + 2 * j + par
            pltpu.make_async_copy(msg.at[frm], codes_all.at[frm], rs_codes.at[frm]).wait()

    def compute(steps):
        code_list = []
        node_list = []
        stat_list = []
        for dx, dy in steps:
            for which in range(2):
                par = k * (1 - which) + (1 - k) * which
                px, quarter, p = piece_at(dx, dy, par)
                if dy == 0:
                    wait_codes(px, par)
                if which == 1:
                    wait_piece(p)
                half = lax.div(quarter, 2)
                lanes = pl.ds(pl.multiple_of(lax.rem(quarter, 2) * QUARTER, 128), QUARTER)
                for j in range(4):
                    frm = px * Z + 2 * j + par
                    code_list.append(codes_all[frm, half, :, lanes].astype(F32))
                    pair = codes_all[frm, 2, :, lanes].astype(F32)
                    node_list.append(jnp.where(half == 0, pair[0:1], pair[1:2]))
                    stat_list.append(pieces[p, j])
        code = jnp.concatenate(code_list, axis=1).astype(jnp.int32)
        nodes = jnp.concatenate(node_list, axis=1).astype(jnp.int32)
        stat = jnp.concatenate(stat_list, axis=1).astype(F32)
        width = code.shape[1]
        bin_iota = lax.broadcasted_iota(jnp.int32, (BINS, width), 0)
        onehot = jnp.concatenate(
            [jnp.where(code[f : f + 1] == bin_iota, 1.0, 0.0).astype(BF16) for f in range(OWNED)],
            axis=0,
        )
        spread = jnp.concatenate(
            [jnp.where(nodes == n, stat, 0.0).astype(BF16) for n in range(NODES)], axis=0
        )
        acc[...] += lax.dot_general(spread, onehot, CONTRACT_LAST, preferred_element_type=F32)

    for what, *at in PLAN:
        if what == "sums":
            client_sums()
        elif what == "near":
            dx, dy = at
            wait_piece(piece_at(dx, dy, k)[2])
            for core in range(2):

                @pl.when(k == core)
                def _():
                    piece_sends(*((dx, dy) if core == 0 else (dy, dx)))

        elif what == "codes":
            for dz in (0, 4, 3, 5, 2, 6, 1, 7):
                codes_copy(2, dz).start()
        elif what == "meet":
            meet_nodes()
        elif what == "take":
            event(*at)
        else:
            compute(list(zip(at[::2], at[1::2])))

    many(node_sums, FEATS - 1, ss_node, rs_node).wait_recv()
    total = jnp.concatenate([node_sums[n] for n in range(NODES)], axis=0)
    left = total[:, :CH]
    whole = total[:, CH : 2 * CH]
    right = whole - left
    left_weight = -left[:, :TARGETS] / (left[:, TARGETS:] + reg_lambda)
    right_weight = -right[:, :TARGETS] / (right[:, TARGETS:] + reg_lambda)
    rows = []
    for n in range(NODES):
        rows.append(left_weight[n : n + 1])
        rows.append(right_weight[n : n + 1])
    weights = jnp.concatenate(rows, axis=0)
    leaf_out[...] = weights
    columns = jnp.concatenate([weights, jnp.zeros((2 * NODES, 128 - TARGETS), F32)], axis=1).T
    child_iota = lax.broadcasted_iota(jnp.int32, (2 * NODES, ROWS), 0)
    child_mask = jnp.where(child_iota == child_ref[...], 1.0, 0.0).astype(BF16)
    lookup = dot3(columns[:TARGETS, :], child_mask)
    margins_out[...] = margins[...] + step_eta * lookup

    row_bin = lax.broadcasted_iota(jnp.int32, (BINS, BINS), 0)
    col_bin = lax.broadcasted_iota(jnp.int32, (BINS, BINS), 1)
    upto = jnp.where(row_bin <= col_bin, 1.0, 0.0).astype(BF16)
    for f in range(OWNED):
        prefix = dot3(acc[:, f * BINS : (f + 1) * BINS], upto)
        for n in range(NODES):
            gl = prefix[n * CH : n * CH + TARGETS]
            hl = prefix[n * CH + TARGETS : (n + 1) * CH]
            g = gl[:, BINS - 1 :]
            h = hl[:, BINS - 1 :]
            value = gl * gl / (hl + reg_lambda)
            value = value + (g - gl) * (g - gl) / (h - hl + reg_lambda)
            value = value - g * g / (h + reg_lambda)
            gains_out[n, f : f + 1, :] = 0.5 * jnp.sum(value, axis=0, keepdims=True)

    @pl.when(k == kp)
    def _():
        for j in range(1, Z):
            z_copy(j).wait_send()

    many(sides, FEATS - 1, ss_side, rs_side).wait_send()
    many(node_sums, FEATS - 1, ss_node, rs_node).wait_send()
    many(sums, CLIENTS - 1, ss_sums, rs_sums).wait_send()
    many(msg, CLIENTS - 1, ss_codes, rs_codes.at[0]).wait_send()
    many(pieces, 2 * X * Y - 1, ss_piece, rs_piece.at[0]).wait_send()


def put_out(gains, leaf, new, gains_out, leaf_out, new_out, sems):
    copies = [
        pltpu.make_async_copy(src, dst, sems.at[i])
        for i, (src, dst) in enumerate(((gains, gains_out), (leaf, leaf_out), (new, new_out)))
    ]
    for copy in copies:
        copy.start()
    for copy in copies:
        copy.wait()


def local(bin_codes, node_ids, margins, labels, split_feature, split_bin):
    vmem = pl.BlockSpec(memory_space=pltpu.VMEM)
    hbm = pl.BlockSpec(memory_space=pltpu.HBM)
    dma = pltpu.SemaphoreType.DMA
    shapes = (
        jax.ShapeDtypeStruct((NODES, OWNED, BINS), F32),
        jax.ShapeDtypeStruct((2 * NODES, TARGETS), F32),
        jax.ShapeDtypeStruct((TARGETS, ROWS), F32),
    )
    outs = pl.pallas_call(
        kernel,
        out_shape=shapes,
        in_specs=[hbm] * 6,
        out_specs=(vmem, vmem, vmem),
        scratch_shapes=[
            pltpu.SMEM((NODES,), jnp.int32),
            pltpu.SMEM((NODES,), jnp.int32),
            pltpu.VMEM((SLAB, ROWS), jnp.int32),
            pltpu.VMEM((ROWS // 128, 128), jnp.int32),
            pltpu.VMEM((TARGETS, ROWS), F32),
            pltpu.VMEM((TARGETS, ROWS), F32),
            dma((6,)),
            pltpu.VMEM((CLIENTS, 3, 2, HALF), BF16),
            pltpu.VMEM((CLIENTS, 3, 2, HALF), BF16),
            pltpu.VMEM((CH, ROWS), BF16),
            pltpu.VMEM((2 * X * Y, 4, CH, QUARTER), BF16),
            pltpu.VMEM((FEATS, 2, HALF), BF16),
            pltpu.VMEM((1, ROWS), jnp.int32),
            pltpu.VMEM((2 * NODES, 128), F32),
            pltpu.VMEM((CLIENTS, 1, 128), F32),
            pltpu.VMEM((FEATS, 1, 128), F32),
            pltpu.VMEM((NODES * CH, OWNED * BINS), F32),
            pltpu.SemaphoreType.REGULAR,
            dma,
            dma((CLIENTS,)),
            dma,
            dma,
            dma,
            dma,
            dma,
            dma,
            dma((Z,)),
            dma((4,)),
            dma,
            dma((2 * X * Y,)),
        ],
        compiler_params=pltpu.CompilerParams(
            collective_id=0, has_side_effects=True, vmem_limit_bytes=36 << 20
        ),
        name="level",
    )(*[pltpu.with_memory_space_constraint(a, pltpu.HBM) for a in (split_feature, split_bin, bin_codes, node_ids.reshape(ROWS // 128, 128), margins, labels)])
    return pl.pallas_call(
        put_out,
        out_shape=shapes,
        in_specs=[vmem] * 3,
        out_specs=(hbm,) * 3,
        scratch_shapes=[dma((3,))],
        compiler_params=pltpu.CompilerParams(vmem_limit_bytes=4 << 20),
        name="put_out",
    )(*outs)


def solution(mesh):
    in_specs = (P("feat", "client"), P("client"), P(None, "client"), P(None, "client"), P(), P())
    out_specs = (P(None, ("feat", "client"), None), P(), P(None, "client"))
    return jax.shard_map(local, mesh=mesh, in_specs=in_specs, out_specs=out_specs, check_vma=False)
```

```python
import jax
import jax.numpy as jnp
from jax import lax
from jax.experimental import pallas as pl
from jax.experimental.pallas import tpu as pltpu
from jax.sharding import PartitionSpec as P

F32 = jnp.float32
BF16 = jnp.bfloat16
MESH = pl.DeviceIdType.MESH
BINS = 256
NODES = 8
TARGETS = 16
CH = 2 * TARGETS
X, Y, Z = 4, 4, 8
CLIENTS = X * Z
FEATS = 2 * Y
ROWS = 1536
QUARTER = ROWS // Y
HALF = ROWS // 2
SLAB = 64
OWNED = 2
reg_lambda = 1.0
step_eta = 0.5
PLAN = (
    ("add", 0, 0), ("sums",), ("near", 0, 1), ("near", 0, 3), ("near", 1, 0), ("near", 3, 0),
    ("add", 0, 1, 0, 3), ("codes",), ("add", 1, 0, 3, 0), ("take", 2, 0), ("take", 1, 1), ("take", 1, 3),
    ("take", 3, 1), ("take", 3, 3), ("add", 1, 1, 1, 3), ("take", 0, 2), ("add", 3, 1, 3, 3),
    ("take", 2, 1), ("take", 2, 3), ("meet",), ("add", 0, 2, 2, 0), ("take", 1, 2), ("take", 3, 2),
    ("add", 1, 2, 3, 2), ("leaf",), ("take", 2, 2), ("add", 2, 1, 2, 3), ("add", 2, 2),
)
CONTRACT_LAST = (((1,), (1,)), ((), ()))


def split3(a):
    hi = a.astype(BF16)
    rest = a - hi.astype(F32)
    mid = rest.astype(BF16)
    low = (rest - mid.astype(F32)).astype(BF16)
    return hi, mid, low


def dot3(a, b):
    hi, mid, low = split3(a)
    out = jnp.dot(low, b, preferred_element_type=F32)
    out = out + jnp.dot(mid, b, preferred_element_type=F32)
    return out + jnp.dot(hi, b, preferred_element_type=F32)


def remote(src, dst, send, recv, client, feat):
    return pltpu.make_async_remote_copy(
        src_ref=src,
        dst_ref=dst,
        send_sem=send,
        recv_sem=recv,
        device_id=(client, feat),
        device_id_type=MESH,
    )


def kernel(
    feature_in,
    bin_in,
    codes_in,
    node_in,
    margins_in,
    labels_in,
    gains_out,
    leaf_out,
    margins_out,
    split_feature,
    split_bin,
    codes,
    node_ids,
    margins,
    labels,
    ls,
    msg,
    codes_all,
    stats,
    pieces,
    sides,
    child_ref,
    parts,
    sums,
    node_sums,
    acc,
    far,
    ss_codes,
    rs_codes,
    ss_side,
    rs_side,
    ss_sums,
    rs_sums,
    ss_node,
    rs_node,
    ss_z,
    rs_z,
    ss_piece,
    rs_piece,
):
    me = lax.axis_index("client")
    feat = lax.axis_index("feat")
    x = lax.div(me, Z)
    z = lax.rem(me, Z)
    y = lax.div(feat, 2)
    k = lax.rem(feat, 2)
    kp = lax.rem(z, 2)
    zz_own = lax.div(z, 2)

    barrier = pltpu.get_barrier_semaphore()

    for j in (4, 3, 5, 2, 6, 1, 7):
        pl.semaphore_signal(
            barrier, inc=1, device_id=(x * Z + lax.rem(z + j, Z), feat), device_id_type=MESH
        )
    for j in (2, 1, 3):
        pl.semaphore_signal(
            barrier, inc=1, device_id=((lax.rem(x + j, X)) * Z + z, feat), device_id_type=MESH
        )
    for j in range(1, FEATS):
        pl.semaphore_signal(
            barrier, inc=1, device_id=(me, lax.rem(feat + j, FEATS)), device_id_type=MESH
        )

    loads = [
        pltpu.make_async_copy(src, dst, ls.at[i])
        for i, (src, dst) in enumerate(
            (
                (margins_in, margins),
                (labels_in, labels),
                (node_in, node_ids),
                (codes_in, codes),
                (feature_in, split_feature),
                (bin_in, split_bin),
            )
        )
    ]
    for load in loads:
        load.start()
    for load in loads[:2]:
        load.wait()
    probability = 1.0 / (1.0 + jnp.exp(-margins[...]))
    stats[0:TARGETS, :] = (probability - labels[...]).astype(BF16)
    stats[TARGETS:CH, :] = (probability * (1.0 - probability)).astype(BF16)

    def piece_at(dx, dy, par):
        px = lax.rem(x + dx, X)
        quarter = lax.rem(y + dy, Y)
        return px, quarter, (quarter * X + px) * 2 + par

    first = piece_at(0, 0, k)[2]

    @pl.when(k == kp)
    def _():
        pieces[first, zz_own] = stats[:, pl.ds(pl.multiple_of(y * QUARTER, 128), QUARTER)]

    pl.semaphore_wait(barrier, Z - 1 + X - 1 + FEATS - 1)

    def z_copy(j):
        to = lax.rem(z + j, Z)
        return remote(
            pieces.at[first, zz_own],
            pieces.at[first, zz_own],
            ss_z.at[to],
            rs_z.at[zz_own],
            x * Z + to,
            feat,
        )

    @pl.when(k == kp)
    def _():
        for j in (4, 3, 5, 2, 6, 1, 7):
            z_copy(j).start()

    for load in loads[2:]:
        load.wait()
    node = jnp.concatenate([node_ids[i : i + 1, :] for i in range(ROWS // 128)], axis=1)

    node_f = node.astype(F32)
    node_pair = jnp.concatenate([node_f[:, :HALF], node_f[:, HALF:]], axis=0).astype(BF16)

    def fill(q, carry):
        block = codes[pl.ds(pl.multiple_of(8 * q, 8), 8), :].astype(F32)
        for i in range(4):
            pair = block[OWNED * i : OWNED * (i + 1)].astype(BF16)
            msg[4 * q + i, 0] = pair[:, :HALF]
            msg[4 * q + i, 1] = pair[:, HALF:]
            msg[4 * q + i, 2] = node_pair
        return carry

    lax.fori_loop(0, CLIENTS // 4, fill, 0)

    side = jnp.zeros((1, ROWS), F32)
    for n in range(NODES):
        column = split_feature[n] - feat * SLAB
        held = jnp.where((column >= 0) & (column < SLAB), 1.0, 0.0)
        row = codes[pl.ds(jnp.clip(column, 0, SLAB - 1), 1), :]
        right = jnp.where((row > split_bin[n]) & (node == n), 1.0, 0.0)
        side = side + held * right
    sides[feat] = jnp.concatenate([side[:, :HALF], side[:, HALF:]], axis=0).astype(BF16)

    def codes_copy(dx, dz):
        to = lax.rem(x + dx, X) * Z + lax.rem(z + dz, Z)
        return remote(msg.at[to], codes_all.at[me], ss_codes, rs_codes.at[me], to, feat)

    for j in (4, 3, 5, 2, 6, 1, 7):
        codes_copy(0, j).start()
    for j in range(1, Z):
        pl.semaphore_signal(
            far, inc=1, device_id=(x * Z + lax.rem(z + j, Z), feat), device_id_type=MESH
        )

    def side_copy(j):
        to = lax.rem(feat + j, FEATS)
        return remote(sides.at[feat], sides.at[feat], ss_side, rs_side, me, to)

    for j in range(1, FEATS):
        side_copy(j).start()
    own_codes = pltpu.make_async_copy(msg.at[me], codes_all.at[me], rs_codes.at[me])
    own_codes.start()
    def along(da, db):
        ax = da * (1 - k) + db * k
        ay = da * k + db * (1 - k)
        return (lax.rem(x + ax, X)) * Z + z, (lax.rem(y + ay, Y)) * 2 + k

    def piece_copy(p, client, to_feat):
        return remote(pieces.at[p], pieces.at[p], ss_piece, rs_piece.at[p], client, to_feat)

    def own_piece(ra, rb):
        return piece_at(ra * (1 - k) + rb * k, ra * k + rb * (1 - k), k)[2]

    def piece_sends(ra, rb):
        p = own_piece(ra, rb)
        to = []
        if rb == 0 and ra == 0:
            to += [(1, 0), (3, 0), (2, 0)]
        if rb == 0:
            to += [(0, 1), (0, 3)]
        if rb == 3 and ra in (1, 2):
            to += [(0, 1)]
        if rb == 1 and ra in (0, 3):
            to += [(0, 3)]
        for da, db in to:
            piece_copy(p, *along(da, db)).start()
        piece_copy(p, me, y * 2 + (1 - k)).start()

    def wait_piece(p):
        remote(
            pieces.at[p], pieces.at[p], ss_piece, rs_piece.at[p], me, y * 2 + (1 - k)
        ).wait_recv()

    for j in range(4):

        @pl.when(2 * j + k != z)
        def _():
            remote(
                pieces.at[first, j],
                pieces.at[first, j],
                ss_z.at[2 * j + k],
                rs_z.at[j],
                x * Z + 2 * j + k,
                feat,
            ).wait_recv()

    piece_sends(0, 0)
    pl.semaphore_wait(far, Z - 1)

    for dz in (0, 4, 3, 5, 2, 6, 1, 7):
        for dx in (1, 3):
            codes_copy(dx, dz).start()

    def sums_copy(j):
        to = lax.rem(me + j, CLIENTS)
        return remote(sums.at[me], sums.at[me], ss_sums, rs_sums, to, feat)

    def node_copy(j):
        to = lax.rem(feat + j, FEATS)
        return remote(node_sums.at[feat], node_sums.at[feat], ss_node, rs_node, me, to)

    def many(ref, count, send, recv):
        return remote(ref.at[pl.ds(0, count)], ref.at[pl.ds(0, count)], send, recv, me, feat)

    def client_sums():
        many(sides, FEATS - 1, ss_side, rs_side).wait_recv()
        side_pair = sides[0].astype(F32)
        for j in range(1, FEATS):
            side_pair = side_pair + sides[j].astype(F32)
        side = jnp.concatenate([side_pair[0:1], side_pair[1:2]], axis=1)
        child = 2 * node + side.astype(jnp.int32)
        child_ref[...] = child
        node_iota = lax.broadcasted_iota(jnp.int32, (NODES, ROWS), 0)
        left_mask = jnp.where(2 * node_iota == child, 1.0, 0.0)
        node_mask = jnp.where(node_iota == node, 1.0, 0.0)
        mask = jnp.concatenate([left_mask, node_mask], axis=0).astype(BF16)
        part = lax.dot_general(mask, stats[...], CONTRACT_LAST, preferred_element_type=F32)
        parts[...] = jnp.concatenate([part, jnp.zeros((2 * NODES, 128 - CH), F32)], axis=1)
        sums[me] = jnp.concatenate(
            [
                parts[pl.ds(feat, 1), :CH],
                parts[pl.ds(NODES + feat, 1), :CH],
                jnp.zeros((1, 128 - 2 * CH), F32),
            ],
            axis=1,
        )

        for j in range(1, CLIENTS):
            sums_copy(j).start()

    def meet_nodes():
        many(sums, CLIENTS - 1, ss_sums, rs_sums).wait_recv()
        node_sums[feat] = jnp.sum(sums[...], axis=0)
        for j in range(1, FEATS):
            node_copy(j).start()

    def event(ra, rb):
        wait_piece(own_piece(ra, rb))
        piece_sends(ra, rb)

    acc[...] = jnp.zeros_like(acc)

    def wait_codes(px, par):
        for j in range(4):
            frm = px * Z + 2 * j + par
            pltpu.make_async_copy(msg.at[frm], codes_all.at[frm], rs_codes.at[frm]).wait()

    def compute(steps):
        code_list = []
        node_list = []
        stat_list = []
        for dx, dy in steps:
            for which in range(2):
                par = k * (1 - which) + (1 - k) * which
                px, quarter, p = piece_at(dx, dy, par)
                if dy == 0:
                    wait_codes(px, par)
                if which == 1:
                    wait_piece(p)
                half = lax.div(quarter, 2)
                lanes = pl.ds(pl.multiple_of(lax.rem(quarter, 2) * QUARTER, 128), QUARTER)
                for j in range(4):
                    frm = px * Z + 2 * j + par
                    code_list.append(codes_all[frm, half, :, lanes].astype(F32))
                    pair = codes_all[frm, 2, :, lanes].astype(F32)
                    node_list.append(jnp.where(half == 0, pair[0:1], pair[1:2]))
                    stat_list.append(pieces[p, j])
        code = jnp.concatenate(code_list, axis=1).astype(jnp.int32)
        nodes = jnp.concatenate(node_list, axis=1).astype(jnp.int32)
        stat = jnp.concatenate(stat_list, axis=1).astype(F32)
        width = code.shape[1]
        bin_iota = lax.broadcasted_iota(jnp.int32, (BINS, width), 0)
        onehot = jnp.concatenate(
            [jnp.where(code[f : f + 1] == bin_iota, 1.0, 0.0).astype(BF16) for f in range(OWNED)],
            axis=0,
        )
        spread = jnp.concatenate(
            [jnp.where(nodes == n, stat, 0.0).astype(BF16) for n in range(NODES)], axis=0
        )
        acc[...] += lax.dot_general(spread, onehot, CONTRACT_LAST, preferred_element_type=F32)

    def finish_leaves():
        many(node_sums, FEATS - 1, ss_node, rs_node).wait_recv()
        total = jnp.concatenate([node_sums[n] for n in range(NODES)], axis=0)
        left = total[:, :CH]
        whole = total[:, CH : 2 * CH]
        right = whole - left
        left_weight = -left[:, :TARGETS] / (left[:, TARGETS:] + reg_lambda)
        right_weight = -right[:, :TARGETS] / (right[:, TARGETS:] + reg_lambda)
        rows = []
        for n in range(NODES):
            rows.append(left_weight[n : n + 1])
            rows.append(right_weight[n : n + 1])
        weights = jnp.concatenate(rows, axis=0)
        leaf_out[...] = weights
        columns = jnp.concatenate([weights, jnp.zeros((2 * NODES, 128 - TARGETS), F32)], axis=1).T
        child_iota = lax.broadcasted_iota(jnp.int32, (2 * NODES, ROWS), 0)
        child_mask = jnp.where(child_iota == child_ref[...], 1.0, 0.0).astype(BF16)
        lookup = dot3(columns[:TARGETS, :], child_mask)
        margins_out[...] = margins[...] + step_eta * lookup

    for what, *at in PLAN:
        if what == "sums":
            client_sums()
        elif what == "near":
            dx, dy = at
            wait_piece(piece_at(dx, dy, k)[2])
            for core in range(2):

                @pl.when(k == core)
                def _():
                    piece_sends(*((dx, dy) if core == 0 else (dy, dx)))

        elif what == "codes":
            for dz in (0, 4, 3, 5, 2, 6, 1, 7):
                codes_copy(2, dz).start()
        elif what == "meet":
            meet_nodes()
        elif what == "leaf":
            finish_leaves()
        elif what == "take":
            event(*at)
        else:
            compute(list(zip(at[::2], at[1::2])))

    row_bin = lax.broadcasted_iota(jnp.int32, (BINS, BINS), 0)
    col_bin = lax.broadcasted_iota(jnp.int32, (BINS, BINS), 1)
    upto = jnp.where(row_bin <= col_bin, 1.0, 0.0).astype(BF16)
    for f in range(OWNED):
        prefix = dot3(acc[:, f * BINS : (f + 1) * BINS], upto)
        for n in range(NODES):
            gl = prefix[n * CH : n * CH + TARGETS]
            hl = prefix[n * CH + TARGETS : (n + 1) * CH]
            g = gl[:, BINS - 1 :]
            h = hl[:, BINS - 1 :]
            value = gl * gl / (hl + reg_lambda)
            value = value + (g - gl) * (g - gl) / (h - hl + reg_lambda)
            value = value - g * g / (h + reg_lambda)
            gains_out[n, f : f + 1, :] = 0.5 * jnp.sum(value, axis=0, keepdims=True)

    @pl.when(k == kp)
    def _():
        for j in range(1, Z):
            z_copy(j).wait_send()

    many(sides, FEATS - 1, ss_side, rs_side).wait_send()
    many(node_sums, FEATS - 1, ss_node, rs_node).wait_send()
    many(sums, CLIENTS - 1, ss_sums, rs_sums).wait_send()
    many(msg, CLIENTS - 1, ss_codes, rs_codes.at[0]).wait_send()
    many(pieces, 2 * X * Y - 1, ss_piece, rs_piece.at[0]).wait_send()


def put_out(gains, leaf, new, gains_out, leaf_out, new_out, sems):
    copies = [
        pltpu.make_async_copy(src, dst, sems.at[i])
        for i, (src, dst) in enumerate(((gains, gains_out), (leaf, leaf_out), (new, new_out)))
    ]
    for copy in copies:
        copy.start()
    for copy in copies:
        copy.wait()


def local(bin_codes, node_ids, margins, labels, split_feature, split_bin):
    vmem = pl.BlockSpec(memory_space=pltpu.VMEM)
    hbm = pl.BlockSpec(memory_space=pltpu.HBM)
    dma = pltpu.SemaphoreType.DMA
    shapes = (
        jax.ShapeDtypeStruct((NODES, OWNED, BINS), F32),
        jax.ShapeDtypeStruct((2 * NODES, TARGETS), F32),
        jax.ShapeDtypeStruct((TARGETS, ROWS), F32),
    )
    outs = pl.pallas_call(
        kernel,
        out_shape=shapes,
        in_specs=[hbm] * 6,
        out_specs=(vmem, vmem, vmem),
        scratch_shapes=[
            pltpu.SMEM((NODES,), jnp.int32),
            pltpu.SMEM((NODES,), jnp.int32),
            pltpu.VMEM((SLAB, ROWS), jnp.int32),
            pltpu.VMEM((ROWS // 128, 128), jnp.int32),
            pltpu.VMEM((TARGETS, ROWS), F32),
            pltpu.VMEM((TARGETS, ROWS), F32),
            dma((6,)),
            pltpu.VMEM((CLIENTS, 3, 2, HALF), BF16),
            pltpu.VMEM((CLIENTS, 3, 2, HALF), BF16),
            pltpu.VMEM((CH, ROWS), BF16),
            pltpu.VMEM((2 * X * Y, 4, CH, QUARTER), BF16),
            pltpu.VMEM((FEATS, 2, HALF), BF16),
            pltpu.VMEM((1, ROWS), jnp.int32),
            pltpu.VMEM((2 * NODES, 128), F32),
            pltpu.VMEM((CLIENTS, 1, 128), F32),
            pltpu.VMEM((FEATS, 1, 128), F32),
            pltpu.VMEM((NODES * CH, OWNED * BINS), F32),
            pltpu.SemaphoreType.REGULAR,
            dma,
            dma((CLIENTS,)),
            dma,
            dma,
            dma,
            dma,
            dma,
            dma,
            dma((Z,)),
            dma((4,)),
            dma,
            dma((2 * X * Y,)),
        ],
        compiler_params=pltpu.CompilerParams(
            collective_id=0, has_side_effects=True, vmem_limit_bytes=36 << 20
        ),
        name="level",
    )(*[pltpu.with_memory_space_constraint(a, pltpu.HBM) for a in (split_feature, split_bin, bin_codes, node_ids.reshape(ROWS // 128, 128), margins, labels)])
    return pl.pallas_call(
        put_out,
        out_shape=shapes,
        in_specs=[vmem] * 3,
        out_specs=(hbm,) * 3,
        scratch_shapes=[dma((3,))],
        compiler_params=pltpu.CompilerParams(vmem_limit_bytes=4 << 20),
        name="put_out",
    )(*outs)


def solution(mesh):
    in_specs = (P("feat", "client"), P("client"), P(None, "client"), P(None, "client"), P(), P())
    out_specs = (P(None, ("feat", "client"), None), P(), P(None, "client"))
    return jax.shard_map(local, mesh=mesh, in_specs=in_specs, out_specs=out_specs, check_vma=False)
```
